32 devices in a mesh: groups: 2 (over x), gz: 16 (over z, y, core).
Axes of the slice: x: 2, y: 2, z: 4, core: 2. Of those that a mesh axis runs over, the one named last changes fastest.
Arguments:
- labels: int32 [128, 256, 256], P(('groups', 'gz')), parts along dimension 0, may hold values from 0 to 7
- tensor_table: float32 [16, 7], P('groups'), parts along dimension 0, may hold values from -0.3 to 3.5, as said below
- bounds: float32 [4], P('groups'), parts along dimension 0, may hold values from 0 to 51, as said below
- right_side: float32 [128, 256, 256], P(('groups', 'gz')), parts along dimension 0, may hold values from -18 to 18
Outputs:
- solution: float32 [128, 256, 256], P(('groups', 'gz')), parts along dimension 0
- residual: float32 [128, 256, 256], P(('groups', 'gz')), parts along dimension 0
- residual_norm: float32 [2], P('groups'), parts along dimension 0
The draws below stay inside these ranges and needn't reach their ends.
There are 2 independent parts, one for each index of `groups`. The reference program is written for one: setup_inputs(seed, part) draws one part's arguments, and reference() takes and returns one part's arrays. A program takes and returns all parts, laid end to end along the dimension named above; each array names one. Nothing has to cross between parts.
Inputs may be any that keep to these rules, and one draw needn't show every extreme that they name: `tensor_table`: every tensor is diagonally dominant: each diagonal component exceeds the sum of the magnitudes of its row's off-diagonal components by 0.4 or more; reactions are positive. 0 < bounds[0] < bounds[1], and bounds[1] is at least the largest eigenvalue of the operator.
All inputs are finite; a program needn't handle non-finite values.
Results may differ from the reference program's by a relative error of at most 0.00002.
Values sent between devices are 32-bit elements; how exact they have to be, the bound alone decides.
A program may use at most 256 MiB of HBM per device.

```python
import math
import jax
import jax.numpy as jnp

NY = 256
NZ = 256
ITERS = 3
PHASES = 8
NX = 64


def make_table(key):
    inner = jax.random.fold_in(key, 17)
    keys = jax.random.split(inner, 4)
    couplings = jax.random.uniform(keys[0], (PHASES, 3), jnp.float32, -0.3, 0.3)
    magnitude = jnp.abs(couplings)
    row_sums = jnp.stack([magnitude[:, 0] + magnitude[:, 1], magnitude[:, 0] + magnitude[:, 2], magnitude[:, 1] + magnitude[:, 2]], 1)
    excess = jnp.exp(jax.random.uniform(keys[1], (PHASES, 3), jnp.float32, math.log(0.5), math.log(2.5)))
    diagonal = 0.4 + row_sums + excess
    reaction = jnp.exp(jax.random.uniform(keys[2], (PHASES, 1), jnp.float32, math.log(0.005), math.log(0.05)))
    table = jnp.concatenate([diagonal, couplings, reaction], 1)
    return (table, couplings, diagonal - row_sums, reaction, keys[3])


def draw_tensor_table(key, part):
    table, couplings, axis_weights, reaction, spare = make_table(key)
    return table


def draw_bounds(key, part):
    table, couplings, axis_weights, reaction, spare = make_table(key)
    spare_keys = jax.random.split(spare, 2)
    positive = jnp.max(jnp.maximum(couplings, 0.0), 0)
    negative = jnp.max(jnp.maximum(-couplings, 0.0), 0)
    largest = jnp.sum(jnp.max(axis_weights, 0)) + jnp.sum(positive) + jnp.sum(negative)
    gershgorin = jnp.max(reaction) + 4.0 * largest
    upper = gershgorin * jax.random.uniform(spare_keys[0], (), jnp.float32, 1.0, 1.2)
    lower = upper * jnp.exp(jax.random.uniform(spare_keys[1], (), jnp.float32, math.log(0.02), math.log(0.1)))
    return jnp.stack([lower, upper]).astype(jnp.float32)


def draw_right_side(key, part):
    along = jnp.arange(NX, dtype=jnp.float32) / max(NX - 1, 1)
    along = along[:, None, None]
    noise = jnp.clip(jax.random.normal(key, (NX, NY, NZ), jnp.float32), -4.0, 4.0)
    return noise * (1.0 + 2.0 * along)


def plant(values, key, low, high):
    longest = values.shape.index(max(values.shape))
    spots = []
    for shift in (0, 1):
        where = [jax.random.randint(jax.random.fold_in(key, axis), (), 0, length) for axis, length in enumerate(values.shape)]
        where[longest] = (where[longest] + shift) % values.shape[longest]
        spots.append(tuple(where))
    return values.at[spots[0]].set(low).at[spots[1]].set(high)


def setup_inputs(seed: int = 0, part: int = 0) -> dict:
    streams_of = jax.random.split(jax.random.key(seed), 5)
    part_keys = jax.random.split(jax.random.fold_in(streams_of[4], part), 5)
    return {
        "labels": plant(jax.random.randint(part_keys[0], (NX, NY, NZ), 0, PHASES), jax.random.fold_in(part_keys[0], 1), 0, PHASES - 1).astype(jnp.int32),
        "tensor_table": draw_tensor_table(jax.random.fold_in(jax.random.fold_in(streams_of[4], part), 71), part),
        "bounds": draw_bounds(jax.random.fold_in(jax.random.fold_in(streams_of[4], part), 71), part),
        "right_side": draw_right_side(jax.random.fold_in(jax.random.fold_in(streams_of[4], part), 71), part),
    }


lattice_steps = ((1, 0, 0), (0, 1, 0), (0, 0, 1), (1, 1, 0), (1, -1, 0), (1, 0, 1), (1, 0, -1), (0, 1, 1), (0, 1, -1))

def phase_weights(tensor_table):
    k_xx = tensor_table[:, 0]
    k_yy = tensor_table[:, 1]
    k_zz = tensor_table[:, 2]
    k_xy = tensor_table[:, 3]
    k_xz = tensor_table[:, 4]
    k_yz = tensor_table[:, 5]
    weights = [k_xx - jnp.abs(k_xy) - jnp.abs(k_xz), k_yy - jnp.abs(k_xy) - jnp.abs(k_yz), k_zz - jnp.abs(k_xz) - jnp.abs(k_yz), jnp.maximum(k_xy, 0.0), jnp.maximum(-k_xy, 0.0), jnp.maximum(k_xz, 0.0), jnp.maximum(-k_xz, 0.0), jnp.maximum(k_yz, 0.0), jnp.maximum(-k_yz, 0.0)]
    return (weights, tensor_table[:, 6])

def cell_values(per_phase, labels):
    result = jnp.zeros(labels.shape, jnp.float32)
    for phase in range(per_phase.shape[0]):
        result = jnp.where(labels == phase, per_phase[phase], result)
    return result

def shifted(field, shift_x, shift_y, shift_z):
    length, rows, columns = field.shape
    padded = jnp.pad(field, ((0, 0), (1, 1), (1, 1)))
    return padded[1 + shift_x:length - 1 + shift_x, 1 + shift_y:1 + shift_y + rows, 1 + shift_z:1 + shift_z + columns]

def apply_operator(field, weights, reaction):
    middle_field = field[1:-1]
    image = reaction[1:-1] * middle_field
    for which, offset in enumerate(lattice_steps):
        own_weight = weights[which][1:-1]
        for direction_sign in (1, -1):
            step_x = direction_sign * offset[0]
            step_y = direction_sign * offset[1]
            step_z = direction_sign * offset[2]
            neighbour = shifted(field, step_x, step_y, step_z)
            link = 0.5 * (own_weight + shifted(weights[which], step_x, step_y, step_z))
            image = image + link * (middle_field - neighbour)
    return image

def pad_planes(field):
    return jnp.pad(field, ((1, 1), (0, 0), (0, 0)))

def reference(labels, tensor_table, bounds, right_side):
    per_phase, reaction_phase = phase_weights(tensor_table)
    weights = [pad_planes(cell_values(table_column, labels)) for table_column in per_phase]
    reaction = pad_planes(cell_values(reaction_phase, labels))
    lower_bound = bounds[0]
    upper_bound = bounds[1]
    centre = (upper_bound + lower_bound) / 2.0
    spread = (upper_bound - lower_bound) / 2.0
    sigma_ratio = centre / spread
    factor = 1.0 / sigma_ratio
    solution = jnp.zeros_like(right_side)
    residual = right_side
    direction = right_side / centre
    for iteration in range(ITERS):
        solution = solution + direction
        image = apply_operator(pad_planes(direction), weights, reaction)
        residual = residual - image
        new_factor = 1.0 / (2.0 * sigma_ratio - factor)
        direction = new_factor * factor * direction + 2.0 * new_factor / spread * residual
        factor = new_factor
    residual_norm = jnp.sqrt(jnp.sum(residual * residual)).reshape(1)
    return (solution, residual, residual_norm)
```

```python
import functools

import jax
import jax.numpy as jnp
from jax import lax
from jax.experimental import pallas as pl
from jax.experimental.pallas import tpu as pltpu
from jax.sharding import PartitionSpec as P

ITERS = 3
PAD = 8
ROWS = 16
LANES = 128
MESH = pl.DeviceIdType.MESH


def shift_z(t, step):
    count = t.shape[1] // LANES
    lane = lax.broadcasted_iota(jnp.int32, (t.shape[0], LANES), 1)
    parts = [t[:, k * LANES : (k + 1) * LANES] for k in range(count)]
    rolled = [pltpu.roll(part, (LANES - step) % LANES, 1) for part in parts]
    zero = jnp.zeros_like(rolled[0])
    edge = lane == (LANES - 1 if step > 0 else 0)
    result = []
    for k in range(count):
        other = rolled[k + step] if 0 <= k + step < count else zero
        result.append(jnp.where(edge, other, rolled[k]))
    return jnp.concatenate(result, axis=1)


def pos(t):
    return jnp.maximum(t, 0.0)


def neg(t):
    return jnp.maximum(-t, 0.0)


def kernel(
    n, planes, rows, table_ref, bounds_ref, labels_hbm, rhs_hbm,
    solution_hbm, residual_hbm, norm_ref,
    lab, v1, v2, v3, hx, kxy, kxz, hy, hz, kyz, react, coef, diag, res, out_s, out_r,
    weight, partial, gathered, local_sem, out_sem, send_sem, recv_sem, psend, precv,
):
    me = lax.axis_index("gz")
    left, right = me - 1, me + 1
    has_left, has_right = me > 0, me < n - 1
    fields = (v1, v2, v3)
    chunks = rows // ROWS
    body_rows = pl.ds(PAD, rows)

    barrier = pltpu.get_barrier_semaphore()

    def greet(k, carry):
        pl.semaphore_signal(
            barrier, inc=1, device_id={"gz": lax.rem(me + k, n)}, device_id_type=MESH
        )
        return carry

    lax.fori_loop(1, n, greet, 0)

    load_rhs = pltpu.make_async_copy(
        rhs_hbm, v1.at[pl.ds(1, planes), body_rows], local_sem.at[0]
    )
    load_lab = pltpu.make_async_copy(labels_hbm, lab.at[pl.ds(1, planes)], local_sem.at[1])
    load_lab.start()
    load_rhs.start()
    pl.semaphore_wait(barrier, n - 1)

    def views(kind, plane):
        if kind == 0:
            return lab.at[plane]
        return fields[kind - 1].at[plane, body_rows]

    def source(kind, plane):
        if kind == 0:
            return labels_hbm.at[plane]
        if kind == 1:
            return rhs_hbm.at[plane]
        return fields[kind - 1].at[plane + 1, body_rows]

    def to_left(kind):
        return pltpu.make_async_remote_copy(
            src_ref=source(kind, 0),
            dst_ref=views(kind, planes + 1),
            send_sem=send_sem.at[kind, 0],
            recv_sem=recv_sem.at[kind, 0],
            device_id={"gz": left},
            device_id_type=MESH,
        )

    def to_right(kind):
        return pltpu.make_async_remote_copy(
            src_ref=source(kind, planes - 1),
            dst_ref=views(kind, 0),
            send_sem=send_sem.at[kind, 1],
            recv_sem=recv_sem.at[kind, 1],
            device_id={"gz": right},
            device_id_type=MESH,
        )

    def send(kind):
        @pl.when(has_left)
        def _():
            to_left(kind).start()

        @pl.when(has_right)
        def _():
            to_right(kind).start()

    def receive(kind):
        @pl.when(has_left)
        def _():
            to_right(kind).wait_recv()

        @pl.when(has_right)
        def _():
            to_left(kind).wait_recv()

    send(0)
    send(1)

    for phase in range(weight.shape[0]):
        k_xx, k_yy, k_zz, k_xy, k_xz, k_yz, m = [table_ref[phase, c] for c in range(7)]
        weight[phase, 0] = 0.5 * (k_xx - jnp.abs(k_xy) - jnp.abs(k_xz))
        weight[phase, 1] = 0.5 * (k_yy - jnp.abs(k_xy) - jnp.abs(k_yz))
        weight[phase, 2] = 0.5 * (k_zz - jnp.abs(k_xz) - jnp.abs(k_yz))
        weight[phase, 3] = 0.5 * k_xy
        weight[phase, 4] = 0.5 * k_xz
        weight[phase, 5] = 0.5 * k_yz
        weight[phase, 6] = m

    columns = v1.shape[2]
    strip = jnp.zeros((PAD, columns), jnp.float32)
    for ref in (v1, v2, v3, kxy, hy, kyz):
        for plane in range(ref.shape[0]):
            ref[plane, pl.ds(0, PAD)] = strip
            ref[plane, pl.ds(PAD + rows, PAD)] = strip

    def clear(plane):
        zero = jnp.zeros((ROWS, columns), jnp.float32)

        def step(k, carry):
            at = pl.multiple_of(k * ROWS, ROWS)
            for ref in (v1, v2, v3, kxy):
                ref[plane, pl.ds(at + PAD, ROWS)] = zero
            for ref in (hx, kxz):
                ref[plane, pl.ds(at, ROWS)] = zero
            return carry

        lax.fori_loop(0, chunks, step, 0)

    @pl.when(me == 0)
    def _():
        clear(0)

    @pl.when(me == n - 1)
    def _():
        clear(planes + 1)

    def look_up(plane, at, which):
        label = lab[plane, pl.ds(at, ROWS)]
        bits = [(label & b) != 0 for b in (1, 2, 4)]
        out = []
        for column in which:
            level = [
                jnp.full(label.shape, weight[phase, column], jnp.float32)
                for phase in range(8)
            ]
            for bit in bits:
                level = [
                    jnp.where(bit, level[2 * k + 1], level[2 * k])
                    for k in range(len(level) // 2)
                ]
            out.append(level[0])
        return out

    def look_up_x(plane, at):
        hx[plane, pl.ds(at, ROWS)], kxy[plane, pl.ds(at + PAD, ROWS)], kxz[
            plane, pl.ds(at, ROWS)
        ] = look_up(plane, at, (0, 3, 4))

    def own_step(k, carry):
        at = pl.multiple_of(k * ROWS, ROWS)
        for plane in range(planes):
            values = look_up(plane + 1, at, range(7))
            hx[plane + 1, pl.ds(at, ROWS)] = values[0]
            hy[plane, pl.ds(at + PAD, ROWS)] = values[1]
            hz[plane, pl.ds(at, ROWS)] = values[2]
            kxy[plane + 1, pl.ds(at + PAD, ROWS)] = values[3]
            kxz[plane + 1, pl.ds(at, ROWS)] = values[4]
            kyz[plane, pl.ds(at + PAD, ROWS)] = values[5]
            react[plane, pl.ds(at, ROWS)] = values[6]
        return carry

    def three(ref, plane, at):
        wide = ref[plane, pl.ds(at, ROWS + 2 * PAD)]
        total = ROWS + 2 * PAD
        return (
            wide[PAD : PAD + ROWS],
            pltpu.roll(wide, total - 1, 0)[PAD : PAD + ROWS],
            pltpu.roll(wide, 1, 0)[PAD : PAD + ROWS],
        )

    def coefficients(which):
        def step(k, carry):
            at = pl.multiple_of(k * ROWS, ROWS)
            here = pl.ds(at, ROWS)
            for x in which:
                hx0 = hx[x + 1, here]
                hy0, hyp, hym = three(hy, x, at)
                hz0 = hz[x, here]
                k0 = kxy[x + 1, pl.ds(at + PAD, ROWS)]
                _, kpp, kpm = three(kxy, x + 2, at)
                _, kmp, kmm = three(kxy, x, at)
                xz0, xzp, xzm = kxz[x + 1, here], kxz[x + 2, here], kxz[x, here]
                yz0, yzp, yzm = three(kyz, x, at)
                c = [
                    hx0 + hx[x + 2, here],
                    hx0 + hx[x, here],
                    hy0 + hyp,
                    hy0 + hym,
                    pos(k0) + pos(kpp),
                    pos(k0) + pos(kmm),
                    neg(k0) + neg(kpm),
                    neg(k0) + neg(kmp),
                ]
                total = react[x, here] + 2.0 * (hz0 + jnp.abs(xz0) + jnp.abs(yz0))
                for value in c:
                    total = total + value
                for sign, f, g in ((1, pos, neg), (-1, neg, pos)):
                    ends = [hz0, f(xzp), g(xzm), f(yzp), g(yzm)]
                    hz_s, xz_s, yz_s = [shift_z(t, -sign) for t in (hz0, xz0, yz0)]
                    starts = [hz_s, f(xz_s), g(xz_s), f(yz_s), g(yz_s)]
                    c += [a + b for a, b in zip(starts, ends)]
                    total = total + shift_z(sum(ends[1:], ends[0]), sign)
                for index, value in enumerate(c):
                    coef[index, x, here] = value
                diag[x, here] = total
            return carry

        lax.fori_loop(0, chunks, step, 0)

    def image(loaded, at, x):
        here = pl.ds(at, ROWS)
        u, up, um = loaded(x + 2)
        v, vp, vm = loaded(x + 1)
        w, wp, wm = loaded(x)
        flat = (u, w, vp, vm, up, wm, um, wp)
        side = (v, u, w, vp, vm)
        parts = [
            functools.reduce(
                lambda a, b: a + b,
                [coef[first + i, x, here] * t for i, t in enumerate(terms)],
            )
            for first, terms in ((0, flat), (8, side), (13, side))
        ]
        return (
            diag[x, here] * v - parts[0] - shift_z(parts[1], 1) - shift_z(parts[2], -1)
        ), v

    lower, upper = bounds_ref[0], bounds_ref[1]
    shape = (ROWS, columns)
    centre = jnp.full(shape, (upper + lower) / 2.0)
    spread = jnp.full(shape, (upper - lower) / 2.0)
    inverse = 1.0 / centre
    sigma = centre / spread
    factor = 1.0 / sigma
    factors = []
    for _ in range(ITERS - 1):
        new_factor = 1.0 / (2.0 * sigma - factor)
        factors.append((new_factor * factor, 2.0 * new_factor / spread))
        factor = new_factor

    def iterate(iteration, which, total):
        field = fields[iteration]

        def step(k, total):
            at = pl.multiple_of(k * ROWS, ROWS)
            here = pl.ds(at, ROWS)
            inner = pl.ds(at + PAD, ROWS)
            held = {}

            def loaded(plane):
                if plane not in held:
                    held[plane] = three(field, plane, at)
                return held[plane]

            for x in which:
                picture, v = image(loaded, at, x)
                if iteration == 0:
                    residual = v - picture * inverse
                    direction = v * inverse
                else:
                    residual = res[x, here] - picture
                    direction = v
                if iteration < ITERS - 1:
                    res[x, here] = residual
                    a, b = factors[iteration]
                    fields[iteration + 1][x + 1, inner] = a * direction + b * residual
                else:
                    out_r[x, here] = residual
                    out_s[x, here] = v1[x + 1, inner] * inverse + v2[x + 1, inner] + v
                    total = total + residual * residual
            return total

        return lax.fori_loop(0, chunks, step, total)

    nothing = jnp.zeros(shape, jnp.float32)
    interior = range(1, planes - 1)
    edges = (0, planes - 1)

    load_lab.wait()
    lax.fori_loop(0, chunks, own_step, 0)
    coefficients(interior)
    load_rhs.wait()
    iterate(0, interior, 0)

    receive(0)
    for present, plane in ((has_left, 0), (has_right, planes + 1)):

        @pl.when(present)
        def _():
            def step(k, carry):
                look_up_x(plane, pl.multiple_of(k * ROWS, ROWS))
                return carry

            lax.fori_loop(0, chunks, step, 0)

    coefficients(edges)
    receive(1)
    iterate(0, edges, 0)
    send(2)
    iterate(1, interior, 0)
    receive(2)
    iterate(1, edges, 0)
    send(3)
    total = iterate(2, interior, nothing)

    def put(x):
        return [
            pltpu.make_async_copy(src.at[x], dst.at[x], out_sem.at[which, x])
            for which, (src, dst) in enumerate(((out_s, solution_hbm), (out_r, residual_hbm)))
        ]

    for x in interior:
        for copy in put(x):
            copy.start()
    receive(3)
    total = iterate(2, edges, total)
    for x in edges:
        for copy in put(x):
            copy.start()

    tile = jnp.zeros((8, LANES), jnp.float32)
    for r in range(ROWS // 8):
        for c in range(columns // LANES):
            tile = tile + total[r * 8 : (r + 1) * 8, c * LANES : (c + 1) * LANES]
    partial[...] = tile
    gathered[me] = tile

    def share(k):
        return pltpu.make_async_remote_copy(
            src_ref=partial,
            dst_ref=gathered.at[me],
            send_sem=psend.at[k],
            recv_sem=precv.at[me],
            device_id={"gz": lax.rem(me + k, n)},
            device_id_type=MESH,
        )

    def arrival(k):
        other = lax.rem(me + k, n)
        return pltpu.make_async_remote_copy(
            src_ref=partial,
            dst_ref=gathered.at[other],
            send_sem=psend.at[k],
            recv_sem=precv.at[other],
            device_id={"gz": other},
            device_id_type=MESH,
        )

    def start_share(k, carry):
        share(k).start()
        return carry

    def end_share(k, carry):
        arrival(k).wait_recv()
        return carry

    def end_send(k, carry):
        share(k).wait_send()
        return carry

    lax.fori_loop(1, n, start_share, 0)
    for kind in range(ITERS + 1):

        @pl.when(has_left)
        def _():
            to_left(kind).wait_send()

        @pl.when(has_right)
        def _():
            to_right(kind).wait_send()

    lax.fori_loop(1, n, end_share, 0)
    everything = lax.fori_loop(
        0, n, lambda k, t: t + gathered[k], jnp.zeros((8, LANES), jnp.float32)
    )
    squares = jnp.sum(everything)
    norm_ref[0] = jnp.sqrt(jnp.full((8, LANES), squares))[0, 0]
    lax.fori_loop(1, n, end_send, 0)
    for x in range(planes):
        for copy in put(x):
            copy.wait()


def per_device(labels, tensor_table, bounds, right_side):
    n = lax.axis_size("gz")
    planes, rows, columns = right_side.shape
    phases = tensor_table.shape[0]
    f32 = jnp.float32
    padded = rows + 2 * PAD

    def flat(count):
        return pltpu.VMEM((count, rows, columns), f32)

    def tall(count):
        return pltpu.VMEM((count, padded, columns), f32)

    any_spec = pl.BlockSpec(memory_space=pl.ANY)
    smem_spec = pl.BlockSpec(memory_space=pltpu.SMEM)
    return pl.pallas_call(
        functools.partial(kernel, n, planes, rows),
        out_shape=(
            jax.ShapeDtypeStruct(right_side.shape, f32),
            jax.ShapeDtypeStruct(right_side.shape, f32),
            jax.ShapeDtypeStruct((1,), f32),
        ),
        in_specs=[smem_spec, smem_spec, any_spec, any_spec],
        out_specs=(any_spec, any_spec, smem_spec),
        scratch_shapes=[
            pltpu.VMEM((planes + 2, rows, columns), jnp.int32),
            tall(planes + 2),
            tall(planes + 2),
            tall(planes + 2),
            flat(planes + 2),
            tall(planes + 2),
            flat(planes + 2),
            tall(planes),
            flat(planes),
            tall(planes),
            flat(planes),
            pltpu.VMEM((18, planes, rows, columns), f32),
            flat(planes),
            flat(planes),
            flat(planes),
            flat(planes),
            pltpu.SMEM((phases, 7), f32),
            pltpu.VMEM((8, LANES), f32),
            pltpu.VMEM((n, 8, LANES), f32),
            pltpu.SemaphoreType.DMA((2,)),
            pltpu.SemaphoreType.DMA((2, planes)),
            pltpu.SemaphoreType.DMA((ITERS + 1, 2)),
            pltpu.SemaphoreType.DMA((ITERS + 1, 2)),
            pltpu.SemaphoreType.DMA((n,)),
            pltpu.SemaphoreType.DMA((n,)),
        ],
        compiler_params=pltpu.CompilerParams(
            collective_id=0, has_side_effects=True, vmem_limit_bytes=60 * 1024 * 1024
        ),
    )(tensor_table, bounds, labels, right_side)


def solution(mesh):
    return jax.shard_map(
        per_device,
        mesh=mesh,
        in_specs=(
            P(("groups", "gz"), None, None),
            P("groups", None),
            P("groups"),
            P(("groups", "gz"), None, None),
        ),
        out_specs=(P(("groups", "gz"), None, None), P(("groups", "gz"), None, None), P("groups")),
        check_vma=False,
    )
```

```python
import functools

import jax
import jax.numpy as jnp
from jax import lax
from jax.experimental import pallas as pl
from jax.experimental.pallas import tpu as pltpu
from jax.sharding import PartitionSpec as P

ITERS = 3
PAD = 8
ROWS = 16
LANES = 128
PIECES = 4
MESH = pl.DeviceIdType.MESH


def shift_z(t, step):
    count = t.shape[1] // LANES
    lane = lax.broadcasted_iota(jnp.int32, (t.shape[0], LANES), 1)
    parts = [t[:, k * LANES : (k + 1) * LANES] for k in range(count)]
    rolled = [pltpu.roll(part, (LANES - step) % LANES, 1) for part in parts]
    zero = jnp.zeros_like(rolled[0])
    edge = lane == (LANES - 1 if step > 0 else 0)
    result = []
    for k in range(count):
        other = rolled[k + step] if 0 <= k + step < count else zero
        result.append(jnp.where(edge, other, rolled[k]))
    return jnp.concatenate(result, axis=1)


def pos(t):
    return jnp.maximum(t, 0.0)


def neg(t):
    return jnp.maximum(-t, 0.0)


def kernel(
    n, planes, rows, table_ref, bounds_ref, labels_hbm, rhs_hbm,
    solution_hbm, residual_hbm, norm_ref,
    lab, v1, v2, v3, hx, kxy, kxz, hy, hz, kyz, react, coef, diag, res, out_s, out_r,
    weight, partial, gathered, local_sem, out_sem, send_sem, recv_sem, psend, precv,
):
    me = lax.axis_index("gz")
    left, right = me - 1, me + 1
    has_left, has_right = me > 0, me < n - 1
    fields = (v1, v2, v3)
    chunks = rows // ROWS
    body_rows = pl.ds(PAD, rows)
    piece = rows // PIECES

    def span(kind, c):
        lag = ROWS * max(kind - 1, 0)
        low = piece * c - lag if c else 0
        high = piece * (c + 1) - lag if c < PIECES - 1 else rows
        return low, high

    barrier = pltpu.get_barrier_semaphore()

    def greet(k, carry):
        pl.semaphore_signal(
            barrier, inc=1, device_id={"gz": lax.rem(me + k, n)}, device_id_type=MESH
        )
        return carry

    lax.fori_loop(1, n, greet, 0)

    load_rhs = pltpu.make_async_copy(
        rhs_hbm, v1.at[pl.ds(1, planes), body_rows], local_sem.at[0]
    )
    load_lab = pltpu.make_async_copy(labels_hbm, lab.at[pl.ds(1, planes)], local_sem.at[1])
    load_lab.start()
    load_rhs.start()

    def views(kind, plane, c):
        low, high = span(kind, c)
        if kind == 0:
            return lab.at[plane, pl.ds(low, high - low)]
        return fields[kind - 1].at[plane, pl.ds(low + PAD, high - low)]

    def source(kind, plane, c):
        low, high = span(kind, c)
        if kind == 0:
            return labels_hbm.at[plane, pl.ds(low, high - low)]
        if kind == 1:
            return rhs_hbm.at[plane, pl.ds(low, high - low)]
        return fields[kind - 1].at[plane + 1, pl.ds(low + PAD, high - low)]

    def to_left(kind, c):
        return pltpu.make_async_remote_copy(
            src_ref=source(kind, 0, c),
            dst_ref=views(kind, planes + 1, c),
            send_sem=send_sem.at[kind, c, 0],
            recv_sem=recv_sem.at[kind, c, 0],
            device_id={"gz": left},
            device_id_type=MESH,
        )

    def to_right(kind, c):
        return pltpu.make_async_remote_copy(
            src_ref=source(kind, planes - 1, c),
            dst_ref=views(kind, 0, c),
            send_sem=send_sem.at[kind, c, 1],
            recv_sem=recv_sem.at[kind, c, 1],
            device_id={"gz": right},
            device_id_type=MESH,
        )

    def send(*kinds_at):
        @pl.when(has_left)
        def _():
            for kind, c in kinds_at:
                to_left(kind, c).start()

        @pl.when(has_right)
        def _():
            for kind, c in kinds_at:
                to_right(kind, c).start()

    def receive(kind, c):
        @pl.when(has_left)
        def _():
            to_right(kind, c).wait_recv()

        @pl.when(has_right)
        def _():
            to_left(kind, c).wait_recv()

    for phase in range(weight.shape[0]):
        k_xx, k_yy, k_zz, k_xy, k_xz, k_yz, m = [table_ref[phase, c] for c in range(7)]
        weight[phase, 0] = 0.5 * (k_xx - jnp.abs(k_xy) - jnp.abs(k_xz))
        weight[phase, 1] = 0.5 * (k_yy - jnp.abs(k_xy) - jnp.abs(k_yz))
        weight[phase, 2] = 0.5 * (k_zz - jnp.abs(k_xz) - jnp.abs(k_yz))
        weight[phase, 3] = 0.5 * k_xy
        weight[phase, 4] = 0.5 * k_xz
        weight[phase, 5] = 0.5 * k_yz
        weight[phase, 6] = m

    columns = v1.shape[2]
    strip = jnp.zeros((PAD, columns), jnp.float32)
    for ref in (v1, v2, v3, kxy, hy, kyz):
        for plane in range(ref.shape[0]):
            ref[plane, pl.ds(0, PAD)] = strip
            ref[plane, pl.ds(PAD + rows, PAD)] = strip

    def clear(plane):
        zero = jnp.zeros((ROWS, columns), jnp.float32)

        def step(k, carry):
            at = pl.multiple_of(k * ROWS, ROWS)
            for ref in (v1, v2, v3, kxy):
                ref[plane, pl.ds(at + PAD, ROWS)] = zero
            for ref in (hx, kxz):
                ref[plane, pl.ds(at, ROWS)] = zero
            return carry

        lax.fori_loop(0, chunks, step, 0)

    @pl.when(me == 0)
    def _():
        clear(0)

    @pl.when(me == n - 1)
    def _():
        clear(planes + 1)

    pl.semaphore_wait(barrier, n - 1)
    for c in range(PIECES):
        send((0, c), (1, c))

    def look_up(plane, at, which):
        label = lab[plane, pl.ds(at, ROWS)]
        bits = [(label & b) != 0 for b in (1, 2, 4)]
        out = []
        for column in which:
            level = [
                jnp.full(label.shape, weight[phase, column], jnp.float32)
                for phase in range(8)
            ]
            for bit in bits:
                level = [
                    jnp.where(bit, level[2 * k + 1], level[2 * k])
                    for k in range(len(level) // 2)
                ]
            out.append(level[0])
        return out

    def look_up_x(plane, at):
        hx[plane, pl.ds(at, ROWS)], kxy[plane, pl.ds(at + PAD, ROWS)], kxz[
            plane, pl.ds(at, ROWS)
        ] = look_up(plane, at, (0, 3, 4))

    def own_step(k, carry):
        at = pl.multiple_of(k * ROWS, ROWS)
        for plane in range(planes):
            values = look_up(plane + 1, at, range(7))
            hx[plane + 1, pl.ds(at, ROWS)] = values[0]
            hy[plane, pl.ds(at + PAD, ROWS)] = values[1]
            hz[plane, pl.ds(at, ROWS)] = values[2]
            kxy[plane + 1, pl.ds(at + PAD, ROWS)] = values[3]
            kxz[plane + 1, pl.ds(at, ROWS)] = values[4]
            kyz[plane, pl.ds(at + PAD, ROWS)] = values[5]
            react[plane, pl.ds(at, ROWS)] = values[6]
        return carry

    def three(ref, plane, at):
        wide = ref[plane, pl.ds(at, ROWS + 2 * PAD)]
        total = ROWS + 2 * PAD
        return (
            wide[PAD : PAD + ROWS],
            pltpu.roll(wide, total - 1, 0)[PAD : PAD + ROWS],
            pltpu.roll(wide, 1, 0)[PAD : PAD + ROWS],
        )

    def coefficients(which, low, high):
        def step(k, carry):
            at = pl.multiple_of(k * ROWS, ROWS)
            here = pl.ds(at, ROWS)
            for x in which:
                hx0 = hx[x + 1, here]
                hy0, hyp, hym = three(hy, x, at)
                hz0 = hz[x, here]
                k0 = kxy[x + 1, pl.ds(at + PAD, ROWS)]
                _, kpp, kpm = three(kxy, x + 2, at)
                _, kmp, kmm = three(kxy, x, at)
                xz0, xzp, xzm = kxz[x + 1, here], kxz[x + 2, here], kxz[x, here]
                yz0, yzp, yzm = three(kyz, x, at)
                c = [
                    hx0 + hx[x + 2, here],
                    hx0 + hx[x, here],
                    hy0 + hyp,
                    hy0 + hym,
                    pos(k0) + pos(kpp),
                    pos(k0) + pos(kmm),
                    neg(k0) + neg(kpm),
                    neg(k0) + neg(kmp),
                ]
                total = react[x, here] + 2.0 * (hz0 + jnp.abs(xz0) + jnp.abs(yz0))
                for value in c:
                    total = total + value
                for sign, f, g in ((1, pos, neg), (-1, neg, pos)):
                    ends = [hz0, f(xzp), g(xzm), f(yzp), g(yzm)]
                    hz_s, xz_s, yz_s = [shift_z(t, -sign) for t in (hz0, xz0, yz0)]
                    starts = [hz_s, f(xz_s), g(xz_s), f(yz_s), g(yz_s)]
                    c += [a + b for a, b in zip(starts, ends)]
                    total = total + shift_z(sum(ends[1:], ends[0]), sign)
                for index, value in enumerate(c):
                    coef[index, x, here] = value
                diag[x, here] = total
            return carry

        lax.fori_loop(low // ROWS, high // ROWS, step, 0)

    def image(loaded, at, x):
        here = pl.ds(at, ROWS)
        u, up, um = loaded(x + 2)
        v, vp, vm = loaded(x + 1)
        w, wp, wm = loaded(x)
        flat = (u, w, vp, vm, up, wm, um, wp)
        side = (v, u, w, vp, vm)
        parts = [
            functools.reduce(
                lambda a, b: a + b,
                [coef[first + i, x, here] * t for i, t in enumerate(terms)],
            )
            for first, terms in ((0, flat), (8, side), (13, side))
        ]
        return (
            diag[x, here] * v - parts[0] - shift_z(parts[1], 1) - shift_z(parts[2], -1)
        ), v

    lower, upper = bounds_ref[0], bounds_ref[1]
    shape = (ROWS, columns)
    centre = jnp.full(shape, (upper + lower) / 2.0)
    spread = jnp.full(shape, (upper - lower) / 2.0)
    inverse = 1.0 / centre
    sigma = centre / spread
    factor = 1.0 / sigma
    factors = []
    for _ in range(ITERS - 1):
        new_factor = 1.0 / (2.0 * sigma - factor)
        factors.append((new_factor * factor, 2.0 * new_factor / spread))
        factor = new_factor

    def iterate(iteration, which, total, low, high):
        field = fields[iteration]

        def step(k, total):
            at = pl.multiple_of(k * ROWS, ROWS)
            here = pl.ds(at, ROWS)
            inner = pl.ds(at + PAD, ROWS)
            held = {}

            def loaded(plane):
                if plane not in held:
                    held[plane] = three(field, plane, at)
                return held[plane]

            for x in which:
                picture, v = image(loaded, at, x)
                if iteration == 0:
                    residual = v - picture * inverse
                    direction = v * inverse
                else:
                    residual = res[x, here] - picture
                    direction = v
                if iteration < ITERS - 1:
                    res[x, here] = residual
                    a, b = factors[iteration]
                    fields[iteration + 1][x + 1, inner] = a * direction + b * residual
                else:
                    out_r[x, here] = residual
                    out_s[x, here] = v1[x + 1, inner] * inverse + v2[x + 1, inner] + v
                    total = total + residual * residual
            return total

        return lax.fori_loop(low // ROWS, high // ROWS, step, total)

    nothing = jnp.zeros(shape, jnp.float32)
    interior = range(1, planes - 1)
    edges = (0, planes - 1)

    load_lab.wait()
    lax.fori_loop(0, chunks, own_step, 0)
    coefficients(interior, 0, rows)
    load_rhs.wait()
    iterate(0, interior, 0, 0, rows)

    for c in range(PIECES):
        receive(0, c)
        low, high = span(0, c)
        for present, plane in ((has_left, 0), (has_right, planes + 1)):

            @pl.when(present)
            def _():
                def step(k, carry):
                    look_up_x(plane, pl.multiple_of(k * ROWS, ROWS))
                    return carry

                lax.fori_loop(low // ROWS, high // ROWS, step, 0)

        coefficients(edges, *span(2, c))
        receive(1, c)
        iterate(0, edges, 0, *span(2, c))
        send((2, c))
    iterate(1, interior, 0, 0, rows)
    for c in range(PIECES):
        receive(2, c)
        iterate(1, edges, 0, *span(3, c))
        send((3, c))
    total = iterate(2, interior, nothing, 0, rows)

    def put(x):
        return [
            pltpu.make_async_copy(src.at[x], dst.at[x], out_sem.at[which, x])
            for which, (src, dst) in enumerate(((out_s, solution_hbm), (out_r, residual_hbm)))
        ]

    for x in interior:
        for copy in put(x):
            copy.start()
    for c in range(PIECES):
        receive(3, c)
        total = iterate(2, edges, total, *span(4, c))
    for x in edges:
        for copy in put(x):
            copy.start()

    tile = jnp.zeros((8, LANES), jnp.float32)
    for r in range(ROWS // 8):
        for c in range(columns // LANES):
            tile = tile + total[r * 8 : (r + 1) * 8, c * LANES : (c + 1) * LANES]
    partial[...] = tile
    gathered[me] = tile

    def share(k):
        return pltpu.make_async_remote_copy(
            src_ref=partial,
            dst_ref=gathered.at[me],
            send_sem=psend.at[k],
            recv_sem=precv.at[me],
            device_id={"gz": lax.rem(me + k, n)},
            device_id_type=MESH,
        )

    def arrival(k):
        other = lax.rem(me + k, n)
        return pltpu.make_async_remote_copy(
            src_ref=partial,
            dst_ref=gathered.at[other],
            send_sem=psend.at[k],
            recv_sem=precv.at[other],
            device_id={"gz": other},
            device_id_type=MESH,
        )

    def start_share(k, carry):
        share(k).start()
        return carry

    def end_share(k, carry):
        arrival(k).wait_recv()
        return carry

    def end_send(k, carry):
        share(k).wait_send()
        return carry

    lax.fori_loop(1, n, start_share, 0)

    @pl.when(has_left)
    def _():
        for kind in range(ITERS + 1):
            for c in range(PIECES):
                to_left(kind, c).wait_send()

    @pl.when(has_right)
    def _():
        for kind in range(ITERS + 1):
            for c in range(PIECES):
                to_right(kind, c).wait_send()

    lax.fori_loop(1, n, end_share, 0)
    everything = lax.fori_loop(
        0, n, lambda k, t: t + gathered[k], jnp.zeros((8, LANES), jnp.float32)
    )
    squares = jnp.sum(everything)
    norm_ref[0] = jnp.sqrt(jnp.full((8, LANES), squares))[0, 0]
    lax.fori_loop(1, n, end_send, 0)
    for x in range(planes):
        for copy in put(x):
            copy.wait()


def per_device(labels, tensor_table, bounds, right_side):
    n = lax.axis_size("gz")
    planes, rows, columns = right_side.shape
    phases = tensor_table.shape[0]
    f32 = jnp.float32
    padded = rows + 2 * PAD

    def flat(count):
        return pltpu.VMEM((count, rows, columns), f32)

    def tall(count):
        return pltpu.VMEM((count, padded, columns), f32)

    any_spec = pl.BlockSpec(memory_space=pl.ANY)
    smem_spec = pl.BlockSpec(memory_space=pltpu.SMEM)
    return pl.pallas_call(
        functools.partial(kernel, n, planes, rows),
        out_shape=(
            jax.ShapeDtypeStruct(right_side.shape, f32),
            jax.ShapeDtypeStruct(right_side.shape, f32),
            jax.ShapeDtypeStruct((1,), f32),
        ),
        in_specs=[smem_spec, smem_spec, any_spec, any_spec],
        out_specs=(any_spec, any_spec, smem_spec),
        scratch_shapes=[
            pltpu.VMEM((planes + 2, rows, columns), jnp.int32),
            tall(planes + 2),
            tall(planes + 2),
            tall(planes + 2),
            flat(planes + 2),
            tall(planes + 2),
            flat(planes + 2),
            tall(planes),
            flat(planes),
            tall(planes),
            flat(planes),
            pltpu.VMEM((18, planes, rows, columns), f32),
            flat(planes),
            flat(planes),
            flat(planes),
            flat(planes),
            pltpu.SMEM((phases, 7), f32),
            pltpu.VMEM((8, LANES), f32),
            pltpu.VMEM((n, 8, LANES), f32),
            pltpu.SemaphoreType.DMA((2,)),
            pltpu.SemaphoreType.DMA((2, planes)),
            pltpu.SemaphoreType.DMA((ITERS + 1, PIECES, 2)),
            pltpu.SemaphoreType.DMA((ITERS + 1, PIECES, 2)),
            pltpu.SemaphoreType.DMA((n,)),
            pltpu.SemaphoreType.DMA((n,)),
        ],
        compiler_params=pltpu.CompilerParams(
            collective_id=0, has_side_effects=True, vmem_limit_bytes=60 * 1024 * 1024
        ),
    )(tensor_table, bounds, labels, right_side)


def solution(mesh):
    return jax.shard_map(
        per_device,
        mesh=mesh,
        in_specs=(
            P(("groups", "gz"), None, None),
            P("groups", None),
            P("groups"),
            P(("groups", "gz"), None, None),
        ),
        out_specs=(P(("groups", "gz"), None, None), P(("groups", "gz"), None, None), P("groups")),
        check_vma=False,
    )
```

```python
import functools

import jax
import jax.numpy as jnp
from jax import lax
from jax.experimental import pallas as pl
from jax.experimental.pallas import tpu as pltpu
from jax.sharding import PartitionSpec as P

ITERS = 3
PAD = 8
ROWS = 16
LANES = 128
PIECES = 4
MESH = pl.DeviceIdType.MESH


def shift_z(t, step):
    count = t.shape[1] // LANES
    lane = lax.broadcasted_iota(jnp.int32, (t.shape[0], LANES), 1)
    parts = [t[:, k * LANES : (k + 1) * LANES] for k in range(count)]
    rolled = [pltpu.roll(part, (LANES - step) % LANES, 1) for part in parts]
    zero = jnp.zeros_like(rolled[0])
    edge = lane == (LANES - 1 if step > 0 else 0)
    result = []
    for k in range(count):
        other = rolled[k + step] if 0 <= k + step < count else zero
        result.append(jnp.where(edge, other, rolled[k]))
    return jnp.concatenate(result, axis=1)


def pos(t):
    return jnp.maximum(t, 0.0)


def neg(t):
    return jnp.maximum(-t, 0.0)


def kernel(
    n, planes, rows, table_hbm, bounds_hbm, labels_hbm, rhs_hbm,
    out_s, out_r, norm_ref,
    lab, v1, v2, v3, hx, kxy, kxz, hy, hz, kyz, react, coef, diag, res,
    table_ref, bounds_ref, weight, partial, gathered, known, local_sem, send_sem, recv_sem, psend, precv,
):
    me = lax.axis_index("gz")
    left, right = me - 1, me + 1
    has_left, has_right = me > 0, me < n - 1
    fields = (v1, v2, v3)
    chunks = rows // ROWS
    body_rows = pl.ds(PAD, rows)
    piece = rows // PIECES

    def span(kind, c):
        lag = ROWS * max(kind - 1, 0)
        low = piece * c - lag if c else 0
        high = piece * (c + 1) - lag if c < PIECES - 1 else rows
        return low, high

    barrier = pltpu.get_barrier_semaphore()

    @pl.when(has_left)
    def _():
        pl.semaphore_signal(barrier, inc=1, device_id={"gz": left}, device_id_type=MESH)

    @pl.when(has_right)
    def _():
        pl.semaphore_signal(barrier, inc=1, device_id={"gz": right}, device_id_type=MESH)

    distances = []
    while 2 * 2 ** len(distances) < n - 1:
        distances.append(2 * 2 ** len(distances))

    def within(distance):
        below = jnp.where(me - distance >= 0, 1, 0)
        above = jnp.where(me + distance < n, 1, 0)
        return below + above

    def call(round_):
        distance = distances[round_]
        for other in (me - distance, me + distance):

            @pl.when((other >= 0) & (other < n))
            def _():
                pl.semaphore_signal(
                    known.at[round_], inc=1, device_id={"gz": other}, device_id_type=MESH
                )

    def heed(round_):
        pl.semaphore_wait(known.at[round_], within(distances[round_]))

    load_rhs = pltpu.make_async_copy(
        rhs_hbm, v1.at[pl.ds(1, planes), body_rows], local_sem.at[0]
    )
    load_lab = pltpu.make_async_copy(labels_hbm, lab.at[pl.ds(1, planes)], local_sem.at[1])
    load_table = pltpu.make_async_copy(table_hbm, table_ref, local_sem.at[2])
    load_bounds = pltpu.make_async_copy(bounds_hbm, bounds_ref, local_sem.at[3])
    load_table.start()
    load_bounds.start()
    load_lab.start()
    load_rhs.start()

    def views(kind, plane, c):
        low, high = span(kind, c)
        if kind == 0:
            return lab.at[plane, pl.ds(low, high - low)]
        return fields[kind - 1].at[plane, pl.ds(low + PAD, high - low)]

    def source(kind, plane, c):
        low, high = span(kind, c)
        if kind == 0:
            return labels_hbm.at[plane, pl.ds(low, high - low)]
        if kind == 1:
            return rhs_hbm.at[plane, pl.ds(low, high - low)]
        return fields[kind - 1].at[plane + 1, pl.ds(low + PAD, high - low)]

    def to_left(kind, c):
        return pltpu.make_async_remote_copy(
            src_ref=source(kind, 0, c),
            dst_ref=views(kind, planes + 1, c),
            send_sem=send_sem.at[kind, c, 0],
            recv_sem=recv_sem.at[kind, c, 0],
            device_id={"gz": left},
            device_id_type=MESH,
        )

    def to_right(kind, c):
        return pltpu.make_async_remote_copy(
            src_ref=source(kind, planes - 1, c),
            dst_ref=views(kind, 0, c),
            send_sem=send_sem.at[kind, c, 1],
            recv_sem=recv_sem.at[kind, c, 1],
            device_id={"gz": right},
            device_id_type=MESH,
        )

    def send(*kinds_at):
        @pl.when(has_left)
        def _():
            for kind, c in kinds_at:
                to_left(kind, c).start()

        @pl.when(has_right)
        def _():
            for kind, c in kinds_at:
                to_right(kind, c).start()

    def receive(kind, c):
        @pl.when(has_left)
        def _():
            to_right(kind, c).wait_recv()

        @pl.when(has_right)
        def _():
            to_left(kind, c).wait_recv()

    columns = v1.shape[2]
    strip = jnp.zeros((PAD, columns), jnp.float32)
    for ref in (v1, v2, v3, kxy, hy, kyz):
        for plane in range(ref.shape[0]):
            ref[plane, pl.ds(0, PAD)] = strip
            ref[plane, pl.ds(PAD + rows, PAD)] = strip

    def clear(plane):
        zero = jnp.zeros((ROWS, columns), jnp.float32)

        def step(k, carry):
            at = pl.multiple_of(k * ROWS, ROWS)
            for ref in (v1, v2, v3, kxy):
                ref[plane, pl.ds(at + PAD, ROWS)] = zero
            for ref in (hx, kxz):
                ref[plane, pl.ds(at, ROWS)] = zero
            return carry

        lax.fori_loop(0, chunks, step, 0)

    @pl.when(me == 0)
    def _():
        clear(0)

    @pl.when(me == n - 1)
    def _():
        clear(planes + 1)

    pl.semaphore_wait(barrier, within(1))
    for c in range(PIECES):
        send((0, c), (1, c))

    load_table.wait()
    load_bounds.wait()
    for phase in range(weight.shape[0]):
        k_xx, k_yy, k_zz, k_xy, k_xz, k_yz, m = [table_ref[phase, c] for c in range(7)]
        weight[phase, 0] = 0.5 * (k_xx - jnp.abs(k_xy) - jnp.abs(k_xz))
        weight[phase, 1] = 0.5 * (k_yy - jnp.abs(k_xy) - jnp.abs(k_yz))
        weight[phase, 2] = 0.5 * (k_zz - jnp.abs(k_xz) - jnp.abs(k_yz))
        weight[phase, 3] = 0.5 * k_xy
        weight[phase, 4] = 0.5 * k_xz
        weight[phase, 5] = 0.5 * k_yz
        weight[phase, 6] = m

    def look_up(plane, at, which):
        label = lab[plane, pl.ds(at, ROWS)]
        bits = [(label & b) != 0 for b in (1, 2, 4)]
        out = []
        for column in which:
            level = [
                jnp.full(label.shape, weight[phase, column], jnp.float32)
                for phase in range(8)
            ]
            for bit in bits:
                level = [
                    jnp.where(bit, level[2 * k + 1], level[2 * k])
                    for k in range(len(level) // 2)
                ]
            out.append(level[0])
        return out

    def look_up_x(plane, at):
        hx[plane, pl.ds(at, ROWS)], kxy[plane, pl.ds(at + PAD, ROWS)], kxz[
            plane, pl.ds(at, ROWS)
        ] = look_up(plane, at, (0, 3, 4))

    def own_step(k, carry):
        at = pl.multiple_of(k * ROWS, ROWS)
        for plane in range(planes):
            values = look_up(plane + 1, at, range(7))
            hx[plane + 1, pl.ds(at, ROWS)] = values[0]
            hy[plane, pl.ds(at + PAD, ROWS)] = values[1]
            hz[plane, pl.ds(at, ROWS)] = values[2]
            kxy[plane + 1, pl.ds(at + PAD, ROWS)] = values[3]
            kxz[plane + 1, pl.ds(at, ROWS)] = values[4]
            kyz[plane, pl.ds(at + PAD, ROWS)] = values[5]
            react[plane, pl.ds(at, ROWS)] = values[6]
        return carry

    def three(ref, plane, at):
        wide = ref[plane, pl.ds(at, ROWS + 2 * PAD)]
        total = ROWS + 2 * PAD
        return (
            wide[PAD : PAD + ROWS],
            pltpu.roll(wide, total - 1, 0)[PAD : PAD + ROWS],
            pltpu.roll(wide, 1, 0)[PAD : PAD + ROWS],
        )

    def coefficients(which, low, high):
        def step(k, carry):
            at = pl.multiple_of(k * ROWS, ROWS)
            here = pl.ds(at, ROWS)
            for x in which:
                hx0 = hx[x + 1, here]
                hy0, hyp, hym = three(hy, x, at)
                hz0 = hz[x, here]
                k0 = kxy[x + 1, pl.ds(at + PAD, ROWS)]
                _, kpp, kpm = three(kxy, x + 2, at)
                _, kmp, kmm = three(kxy, x, at)
                xz0, xzp, xzm = kxz[x + 1, here], kxz[x + 2, here], kxz[x, here]
                yz0, yzp, yzm = three(kyz, x, at)
                c = [
                    hx0 + hx[x + 2, here],
                    hx0 + hx[x, here],
                    hy0 + hyp,
                    hy0 + hym,
                    pos(k0) + pos(kpp),
                    pos(k0) + pos(kmm),
                    neg(k0) + neg(kpm),
                    neg(k0) + neg(kmp),
                ]
                total = react[x, here] + 2.0 * (hz0 + jnp.abs(xz0) + jnp.abs(yz0))
                for value in c:
                    total = total + value
                for sign, f, g in ((1, pos, neg), (-1, neg, pos)):
                    ends = [hz0, f(xzp), g(xzm), f(yzp), g(yzm)]
                    hz_s, xz_s, yz_s = [shift_z(t, -sign) for t in (hz0, xz0, yz0)]
                    starts = [hz_s, f(xz_s), g(xz_s), f(yz_s), g(yz_s)]
                    c += [a + b for a, b in zip(starts, ends)]
                    total = total + shift_z(sum(ends[1:], ends[0]), sign)
                for index, value in enumerate(c):
                    coef[index, x, here] = value
                diag[x, here] = total
            return carry

        lax.fori_loop(low // ROWS, high // ROWS, step, 0)

    def image(loaded, at, x):
        here = pl.ds(at, ROWS)
        u, up, um = loaded(x + 2)
        v, vp, vm = loaded(x + 1)
        w, wp, wm = loaded(x)
        flat = (u, w, vp, vm, up, wm, um, wp)
        side = (v, u, w, vp, vm)
        parts = [
            functools.reduce(
                lambda a, b: a + b,
                [coef[first + i, x, here] * t for i, t in enumerate(terms)],
            )
            for first, terms in ((0, flat), (8, side), (13, side))
        ]
        return (
            diag[x, here] * v - parts[0] - shift_z(parts[1], 1) - shift_z(parts[2], -1)
        ), v

    lower, upper = bounds_ref[0], bounds_ref[1]
    shape = (ROWS, columns)
    centre = jnp.full(shape, (upper + lower) / 2.0)
    spread = jnp.full(shape, (upper - lower) / 2.0)
    inverse = 1.0 / centre
    sigma = centre / spread
    factor = 1.0 / sigma
    factors = []
    for _ in range(ITERS - 1):
        new_factor = 1.0 / (2.0 * sigma - factor)
        factors.append((new_factor * factor, 2.0 * new_factor / spread))
        factor = new_factor

    def iterate(iteration, which, total, low, high):
        field = fields[iteration]

        def step(k, total):
            at = pl.multiple_of(k * ROWS, ROWS)
            here = pl.ds(at, ROWS)
            inner = pl.ds(at + PAD, ROWS)
            held = {}

            def loaded(plane):
                if plane not in held:
                    held[plane] = three(field, plane, at)
                return held[plane]

            for x in which:
                picture, v = image(loaded, at, x)
                if iteration == 0:
                    residual = v - picture * inverse
                    direction = v * inverse
                else:
                    residual = res[x, here] - picture
                    direction = v
                if iteration < ITERS - 1:
                    res[x, here] = residual
                    a, b = factors[iteration]
                    fields[iteration + 1][x + 1, inner] = a * direction + b * residual
                else:
                    out_r[x, here] = residual
                    out_s[x, here] = v1[x + 1, inner] * inverse + v2[x + 1, inner] + v
                    total = total + residual * residual
            return total

        return lax.fori_loop(low // ROWS, high // ROWS, step, total)

    nothing = jnp.zeros(shape, jnp.float32)
    interior = range(1, planes - 1)
    edges = (0, planes - 1)

    load_lab.wait()
    lax.fori_loop(0, chunks, own_step, 0)
    coefficients(interior, 0, rows)
    load_rhs.wait()
    iterate(0, interior, 0, 0, rows)

    for c in range(PIECES):
        receive(0, c)
        low, high = span(0, c)
        for present, plane in ((has_left, 0), (has_right, planes + 1)):

            @pl.when(present)
            def _():
                def step(k, carry):
                    look_up_x(plane, pl.multiple_of(k * ROWS, ROWS))
                    return carry

                lax.fori_loop(low // ROWS, high // ROWS, step, 0)

        coefficients(edges, *span(2, c))
        receive(1, c)
        iterate(0, edges, 0, *span(2, c))
        send((2, c))
        if c == 0 and distances:
            call(0)
    iterate(1, interior, 0, 0, rows)
    for c in range(PIECES):
        receive(2, c)
        iterate(1, edges, 0, *span(3, c))
        send((3, c))
        if c < len(distances) - 1:
            heed(c)
            call(c + 1)
    for round_ in range(PIECES, len(distances) - 1):
        heed(round_)
        call(round_ + 1)
    total = iterate(2, interior, nothing, 0, rows)

    for c in range(PIECES):
        receive(3, c)
        total = iterate(2, edges, total, *span(4, c))

    tile = jnp.zeros((8, LANES), jnp.float32)
    for r in range(ROWS // 8):
        for c in range(columns // LANES):
            tile = tile + total[r * 8 : (r + 1) * 8, c * LANES : (c + 1) * LANES]
    partial[...] = tile
    gathered[me] = tile

    def share(k):
        return pltpu.make_async_remote_copy(
            src_ref=partial,
            dst_ref=gathered.at[me],
            send_sem=psend.at[k],
            recv_sem=precv.at[me],
            device_id={"gz": lax.rem(me + k, n)},
            device_id_type=MESH,
        )

    def arrival(k):
        other = lax.rem(me + k, n)
        return pltpu.make_async_remote_copy(
            src_ref=partial,
            dst_ref=gathered.at[other],
            send_sem=psend.at[k],
            recv_sem=precv.at[other],
            device_id={"gz": other},
            device_id_type=MESH,
        )

    def start_share(k, carry):
        share(k).start()
        return carry

    def end_share(k, carry):
        arrival(k).wait_recv()
        return carry

    def end_send(k, carry):
        share(k).wait_send()
        return carry

    if distances:
        heed(len(distances) - 1)
    lax.fori_loop(1, n, start_share, 0)

    @pl.when(has_left)
    def _():
        for kind in range(ITERS + 1):
            for c in range(PIECES):
                to_left(kind, c).wait_send()

    @pl.when(has_right)
    def _():
        for kind in range(ITERS + 1):
            for c in range(PIECES):
                to_right(kind, c).wait_send()

    lax.fori_loop(1, n, end_share, 0)
    everything = lax.fori_loop(
        0, n, lambda k, t: t + gathered[k], jnp.zeros((8, LANES), jnp.float32)
    )
    squares = jnp.sum(everything)
    norm_ref[0] = jnp.sqrt(jnp.full((8, LANES), squares))[0, 0]
    lax.fori_loop(1, n, end_send, 0)


def per_device(labels, tensor_table, bounds, right_side):
    n = lax.axis_size("gz")
    planes, rows, columns = right_side.shape
    phases = tensor_table.shape[0]
    f32 = jnp.float32
    padded = rows + 2 * PAD

    def flat(count):
        return pltpu.VMEM((count, rows, columns), f32)

    def tall(count):
        return pltpu.VMEM((count, padded, columns), f32)

    any_spec = pl.BlockSpec(memory_space=pl.ANY)
    vmem_spec = pl.BlockSpec(memory_space=pltpu.VMEM)
    smem_spec = pl.BlockSpec(memory_space=pltpu.SMEM)
    return pl.pallas_call(
        functools.partial(kernel, n, planes, rows),
        out_shape=(
            jax.ShapeDtypeStruct(right_side.shape, f32),
            jax.ShapeDtypeStruct(right_side.shape, f32),
            jax.ShapeDtypeStruct((1,), f32),
        ),
        in_specs=[any_spec] * 4,
        out_specs=(vmem_spec, vmem_spec, smem_spec),
        scratch_shapes=[
            pltpu.VMEM((planes + 2, rows, columns), jnp.int32),
            tall(planes + 2),
            tall(planes + 2),
            tall(planes + 2),
            flat(planes + 2),
            tall(planes + 2),
            flat(planes + 2),
            tall(planes),
            flat(planes),
            tall(planes),
            flat(planes),
            pltpu.VMEM((18, planes, rows, columns), f32),
            flat(planes),
            flat(planes),
            pltpu.SMEM((phases, 7), f32),
            pltpu.SMEM((2,), f32),
            pltpu.SMEM((phases, 7), f32),
            pltpu.VMEM((8, LANES), f32),
            pltpu.VMEM((n, 8, LANES), f32),
            pltpu.SemaphoreType.REGULAR((max(n.bit_length(), 1),)),
            pltpu.SemaphoreType.DMA((4,)),
            pltpu.SemaphoreType.DMA((ITERS + 1, PIECES, 2)),
            pltpu.SemaphoreType.DMA((ITERS + 1, PIECES, 2)),
            pltpu.SemaphoreType.DMA((n,)),
            pltpu.SemaphoreType.DMA((n,)),
        ],
        compiler_params=pltpu.CompilerParams(
            collective_id=0, has_side_effects=True, vmem_limit_bytes=44 * 1024 * 1024
        ),
    )(
        *[
            pltpu.with_memory_space_constraint(array, pltpu.HBM)
            for array in (tensor_table, bounds, labels, right_side)
        ]
    )


def solution(mesh):
    return jax.shard_map(
        per_device,
        mesh=mesh,
        in_specs=(
            P(("groups", "gz"), None, None),
            P("groups", None),
            P("groups"),
            P(("groups", "gz"), None, None),
        ),
        out_specs=(P(("groups", "gz"), None, None), P(("groups", "gz"), None, None), P("groups")),
        check_vma=False,
    )
```
